32 devices in a mesh: row: 16 (over z, x, core), col: 2 (over y).
Axes of the slice: x: 2, y: 2, z: 4, core: 2. Of those that a mesh axis runs over, the one named last changes fastest.
Arguments:
- queries: bfloat16 [16384, 256], P(('row', 'col')), may hold values from -36 to 36
- key_rows: bfloat16 [16384, 128], P(('row', 'col')), may hold values from -16 to 16
- value_rows: bfloat16 [16384, 128], P(('row', 'col')), may hold values from -6 to 6
- out_grad: bfloat16 [16384, 256], P(('row', 'col')), may hold values from -6 to 6
- link_mask: int32 [32, 5], P(('row', 'col')), may hold values 0 or 1
Outputs:
- attention_out: bfloat16 [16384, 256], P(('row', 'col'))
- query_grad: bfloat16 [16384, 256], P(('row', 'col'))
- key_grad: bfloat16 [16384, 128], P(('row', 'col'))
- value_grad: bfloat16 [16384, 128], P(('row', 'col'))
The draws below stay inside these ranges and needn't reach their ends.
All inputs are finite; a program needn't handle non-finite values. No bound on the sum of `link_mask` on one device may be relied on, other than what follows from the above.
Results may differ from the reference program's by a relative error of at most 0.025.
Values may be sent and summed in bfloat16 or wider, within the bound.
No kernel may reach another device: no remote copies, remote signals or barrier semaphores. Data moves between devices by JAX's collectives and lax.ppermute only.
A program may use at most 64 MiB of HBM per device.

```python
import math
import jax
import jax.numpy as jnp
from jax import lax

TOK_DEV = 512
HD = 128
HQ = 2
LEVELS = 5
BLOCKS = 32
SEQ = 16384


def powers_of_two(exponents):
    table = jnp.array([2.0 ** power for power in range(-8, 0)], jnp.float32)
    return table[exponents + 8]


def coded_rows(key, salt, lead_shape, lowest, highest):
    base = jax.random.fold_in(key, salt)
    full_shape = lead_shape + (HD,)
    side_shape = lead_shape + (1,)
    first = jax.random.randint(jax.random.fold_in(base, 1), full_shape, -63, 64, jnp.int32)
    second = jax.random.randint(jax.random.fold_in(base, 2), full_shape, -63, 64, jnp.int32)
    column = jax.random.randint(jax.random.fold_in(base, 3), side_shape, 0, HD, jnp.int32)
    signs = 2 * jax.random.randint(jax.random.fold_in(base, 4), side_shape, 0, 2, jnp.int32) - 1
    exponents = jax.random.randint(jax.random.fold_in(base, 5), side_shape, lowest, highest + 1, jnp.int32)
    columns = jnp.arange(HD, dtype=jnp.int32)
    codes = jnp.where(columns == column, 127 * signs, first + second)
    return (codes, exponents)


def paired_rows(key):
    lowest, highest = (-6, -5)
    key_codes, key_expo = coded_rows(key, 101, (SEQ,), lowest, highest)
    query_codes, query_expo = coded_rows(key, 102, (SEQ, HQ), lowest, highest)
    key_out = key_codes.astype(jnp.float32) * powers_of_two(key_expo)
    query_out = (query_codes.astype(jnp.float32) * powers_of_two(query_expo)).reshape(SEQ, HQ * HD)
    return (key_out, query_out)


def draw_queries(key, part):
    return paired_rows(key)[1].astype(jnp.bfloat16)


def draw_key_rows(key, part):
    return paired_rows(key)[0].astype(jnp.bfloat16)


def set_ends(values, key, least, high):
    extent = values.shape
    spot = [jax.random.randint(jax.random.fold_in(key, axis), (), 0, extent[axis]) for axis in range(len(extent))]
    values = values.at[tuple(spot)].set(least)
    longest = extent.index(max(extent))
    spot[longest] = (spot[longest] + 1) % extent[longest]
    return values.at[tuple(spot)].set(high)


def levels(key, shape, pieces, low, high):
    def one(dim, parts):
        steps = jax.random.uniform(jax.random.fold_in(jax.random.fold_in(key, 6), dim), (parts,), jnp.float32, low / len(pieces), high / len(pieces))
        return jnp.repeat(jnp.exp(steps), shape[dim] // parts).reshape((-1,) + (1,) * (len(shape) - dim - 1))

    level = one(*pieces[0])
    for cut in pieces[1:]:
        level = level * one(*cut)
    return level


def bell_draw(own_key, shape, spread, reach, split=(), kind=jnp.bfloat16):
    result = jax.random.normal(own_key, shape, jnp.float32) * spread
    if len(split) > 0:
        result = levels(own_key, shape, split, -0.22, 0.18) * result
    return jnp.clip(result, min=-reach, max=reach).astype(kind)


def setup_inputs(seed: int = 0) -> dict:
    key_of = jax.random.split(jax.random.key(seed), 6)
    queries = draw_queries(jax.random.fold_in(key_of[5], 71), 0)
    key_rows = draw_key_rows(jax.random.fold_in(key_of[5], 71), 0)
    value_rows = bell_draw(key_of[2], (SEQ, HD), 1.0, 6.0, ((0, 32),))
    out_grad = bell_draw(key_of[3], (SEQ, HQ * HD), 1.0, 6.0, ((0, 32),))
    link_mask = set_ends((jax.random.randint(key_of[4], (BLOCKS, LEVELS), 0, 4) < 3).astype(jnp.int32), jax.random.fold_in(key_of[4], 1), 0, 1)
    return dict(queries=queries, key_rows=key_rows, value_rows=value_rows, out_grad=out_grad, link_mask=link_mask)


scale_eps = 1e-06

def quantize(values):
    largest = lax.optimization_barrier(jnp.max(jnp.abs(values), axis=-1))
    scales = (largest + scale_eps).astype(jnp.bfloat16)
    scaled = values * (127.0 / scales.astype(jnp.float32))[..., None]
    codes = jnp.clip(jnp.floor(scaled + 0.5), -127.0, 127.0).astype(jnp.bfloat16)
    return (codes, scales)

def dequantize(codes, scales):
    return (codes.astype(jnp.float32) * (scales.astype(jnp.float32) / 127.0)[..., None]).astype(jnp.bfloat16)

def score_block(query_codes, query_scales, key_codes, key_scales):
    head_size = key_codes.shape[-1]
    factor = 1.0 / (127.0 * 127.0 * math.sqrt(head_size))
    raw = jnp.einsum('thc,uc->htu', query_codes.astype(jnp.float32), key_codes.astype(jnp.float32))
    row_factor = jnp.transpose(query_scales.astype(jnp.float32) * factor)
    return raw * row_factor[:, :, None] * key_scales.astype(jnp.float32)[None, None, :]

def reference(queries, key_rows, value_rows, out_grad, link_mask):
    score_scale = 1.0 / math.sqrt(HD)
    query_float = queries.astype(jnp.float32).reshape(SEQ, HQ, HD)
    query_codes, query_scales = quantize(query_float)
    query_hat = dequantize(query_codes, query_scales)
    key_codes, key_scales = quantize(key_rows.astype(jnp.float32))
    key_hat = dequantize(key_codes, key_scales)
    grad_float = out_grad.astype(jnp.float32).reshape(SEQ, HQ, HD)
    offsets = [0] + [2 ** level for level in range(LEVELS)]
    positions = jnp.arange(TOK_DEV, dtype=jnp.int32)
    causal = (positions[None, :] <= positions[:, None])[None, :, :]

    def one_block(state, block_id):
        key_sum, value_sum = state
        start = (block_id * TOK_DEV).astype(jnp.int32)
        codes_here = lax.dynamic_slice_in_dim(query_codes, start, TOK_DEV, 0)
        scales_here = lax.dynamic_slice_in_dim(query_scales, start, TOK_DEV, 0)
        hat_here = lax.dynamic_slice_in_dim(query_hat, start, TOK_DEV, 0)
        grad_here = lax.dynamic_slice_in_dim(grad_float, start, TOK_DEV, 0)
        score_list = []
        value_list = []
        hat_list = []
        starts = []
        for position, offset in enumerate(offsets):
            source_start = (jnp.maximum(block_id - offset, 0) * TOK_DEV).astype(jnp.int32)
            starts.append(source_start)
            codes_there = lax.dynamic_slice_in_dim(key_codes, source_start, TOK_DEV, 0)
            scales_there = lax.dynamic_slice_in_dim(key_scales, source_start, TOK_DEV, 0)
            value_list.append(lax.dynamic_slice_in_dim(value_rows, source_start, TOK_DEV, 0))
            hat_list.append(lax.dynamic_slice_in_dim(key_hat, source_start, TOK_DEV, 0))
            block_scores = score_block(codes_here, scales_here, codes_there, scales_there)
            if position == 0:
                allowed = causal
            else:
                allowed = jnp.logical_and(block_id >= offset, link_mask[block_id, position - 1] == 1)
            score_list.append(jnp.where(allowed, block_scores, -jnp.inf))
        all_scores = jnp.concatenate(score_list, axis=2)
        values_all = jnp.concatenate(value_list, axis=0)
        hat_all = jnp.concatenate(hat_list, axis=0)
        row_top = lax.optimization_barrier(jnp.max(all_scores, axis=2))
        weights = jnp.exp(all_scores - row_top[:, :, None])
        total = lax.optimization_barrier(jnp.sum(weights, axis=2))
        mixed = jnp.einsum('htu,uc->thc', weights.astype(jnp.bfloat16).astype(jnp.float32), values_all.astype(jnp.float32))
        attended = (mixed / jnp.transpose(total)[:, :, None]).astype(jnp.bfloat16)
        delta = lax.optimization_barrier(jnp.sum(grad_here * attended.astype(jnp.float32), axis=2))
        probs = weights / total[:, :, None]
        grad_probs = jnp.einsum('thc,uc->htu', grad_here, values_all.astype(jnp.float32))
        grad_scores = (probs * (grad_probs - jnp.transpose(delta)[:, :, None]) * score_scale).astype(jnp.bfloat16)
        query_part = jnp.einsum('htu,uc->thc', grad_scores.astype(jnp.float32), hat_all.astype(jnp.float32))
        key_part = jnp.einsum('htu,thc->uc', grad_scores.astype(jnp.float32), hat_here.astype(jnp.float32))
        value_part = jnp.einsum('htu,thc->uc', probs.astype(jnp.bfloat16).astype(jnp.float32), grad_here)
        for position in range(len(offsets)):
            lower = position * TOK_DEV
            old_key = lax.dynamic_slice_in_dim(key_sum, starts[position], TOK_DEV, 0)
            key_sum = lax.dynamic_update_slice_in_dim(key_sum, old_key + key_part[lower:lower + TOK_DEV], starts[position], 0)
            old_value = lax.dynamic_slice_in_dim(value_sum, starts[position], TOK_DEV, 0)
            value_sum = lax.dynamic_update_slice_in_dim(value_sum, old_value + value_part[lower:lower + TOK_DEV], starts[position], 0)
        return ((key_sum, value_sum), (attended.reshape(TOK_DEV, HQ * HD), query_part.astype(jnp.bfloat16).reshape(TOK_DEV, HQ * HD)))
    initial = (jnp.zeros((SEQ, HD), jnp.float32), jnp.zeros((SEQ, HD), jnp.float32))
    (key_sum, value_sum), (attended_all, query_all) = lax.scan(one_block, initial, jnp.arange(BLOCKS, dtype=jnp.int32))
    attention_out = attended_all.reshape(SEQ, HQ * HD)
    query_grad = query_all.reshape(SEQ, HQ * HD)
    return (attention_out, query_grad, key_sum.astype(jnp.bfloat16), value_sum.astype(jnp.bfloat16))
```

```python
import math

import jax
import jax.numpy as jnp
from jax import lax
from jax.experimental import pallas as pl
from jax.experimental.pallas import tpu as pltpu
from jax.sharding import PartitionSpec as P

AXES = ("row", "col")
SCALE_EPS = 1e-06
LOWEST = -3.0e38
TOP_LANE = 120
FACTOR_LANE = 121
DELTA_LANE = 122


def shifted(value, steps):
    count = lax.axis_size(AXES)
    first, last = max(0, -steps), min(count, count - steps)
    return lax.ppermute(value, AXES, [(source, source + steps) for source in range(first, last)])


def swapped(value, half):
    count = lax.axis_size(AXES)
    pairs = [(source, source + half if source % (2 * half) < half else source - half) for source in range(count)]
    return lax.ppermute(value, AXES, pairs)


def quantize(values):
    largest = jnp.max(jnp.abs(values), axis=-1, keepdims=True)
    scales = (largest + SCALE_EPS).astype(jnp.bfloat16).astype(jnp.float32)
    codes = jnp.clip(jnp.floor(values * (127.0 / scales) + 0.5), -127.0, 127.0)
    return codes, scales


def key_parts(keys):
    codes, scales = quantize(keys.astype(jnp.float32))
    exact = codes * scales
    high = exact.astype(jnp.bfloat16)
    low = (exact - high.astype(jnp.float32)).astype(jnp.bfloat16)
    return high, low


def dot_nt(left, right):
    return lax.dot_general(left, right, (((1,), (1,)), ((), ())), preferred_element_type=jnp.float32)


def dot_nn(left, right):
    return lax.dot_general(left, right, (((1,), (0,)), ((), ())), preferred_element_type=jnp.float32)


def dot_tn(left, right):
    return lax.dot_general(left, right, (((0,), (0,)), ((), ())), preferred_element_type=jnp.float32)


def with_ones(values):
    return jnp.concatenate([values, jnp.ones_like(values)], axis=1)


def lane_of(stats, lane):
    return stats[:, lane : lane + 1]


def put_lane(stats, lane, column):
    lanes = lax.broadcasted_iota(jnp.int32, stats.shape, 1)
    return jnp.where(lanes == lane, column, stats)


def level_scores(codes, key_pair):
    return dot_nt(jnp.concatenate([codes, codes], axis=1), key_pair)


def make_kernels(tokens, head, heads, levels):
    rows = tokens * heads
    tile = min(256, tokens)
    tiles = rows // tile
    score_factor = math.log2(math.e) / (127.0 * 127.0 * math.sqrt(head))
    score_scale = 1.0 / math.sqrt(head)
    vmem = pl.BlockSpec(memory_space=pltpu.VMEM)
    smem = pl.BlockSpec(memory_space=pltpu.SMEM)
    f32, bf16 = jnp.float32, jnp.bfloat16

    def own_forward(q_ref, kv_ref, codes_ref, hat_ref, w_ref, acc_ref, stats_ref):
        high, low = key_parts(kv_ref[:, :head])
        key_pair = jnp.concatenate([high, low], axis=1)
        values = with_ones(kv_ref[:, head:])
        for index in range(tiles):
            at = pl.ds(index * tile, tile)
            which, start = divmod(index * tile, tokens)
            raw = q_ref[pl.ds(start, tile), which * head : (which + 1) * head].astype(f32)
            codes, scales = quantize(raw)
            hat_ref[at, :] = (codes * (scales / 127.0)).astype(bf16)
            codes = codes.astype(bf16)
            codes_ref[at, :] = codes
            factor = scales * score_factor
            scores = level_scores(codes, key_pair)
            t = lax.broadcasted_iota(jnp.int32, scores.shape, 0) + start
            u = lax.broadcasted_iota(jnp.int32, scores.shape, 1)
            scores = jnp.where(u <= t, scores, LOWEST)
            top = jnp.max(scores, axis=1, keepdims=True)
            weights = jnp.exp2((scores - top) * factor).astype(bf16)
            w_ref[at, :] = weights
            acc_ref[at, :] = dot_nn(weights, values)
            stats = jnp.zeros((tile, 128), f32)
            stats = put_lane(stats, levels, top)
            stats = put_lane(stats, TOP_LANE, top)
            stats = put_lane(stats, FACTOR_LANE, factor)
            stats_ref[at, :] = stats

    def add_levels(which_levels, allowed_ref, codes, stats, acc, key_pairs, values, w_refs, at):
        factor = lane_of(stats, FACTOR_LANE)
        top = lane_of(stats, TOP_LANE)
        for level, key_pair, value, w_ref in zip(which_levels, key_pairs, values, w_refs):
            scores = level_scores(codes, key_pair)
            here = jnp.max(scores, axis=1, keepdims=True)
            weights = jnp.exp2((scores - here) * factor).astype(bf16)
            w_ref[at, :] = weights
            part = dot_nn(weights, value)
            allowed = allowed_ref[level] == 1
            new_top = jnp.maximum(top, jnp.where(allowed, here, LOWEST))
            grow = jnp.where(allowed, jnp.exp2((here - new_top) * factor), 0.0)
            acc = acc * jnp.exp2((top - new_top) * factor) + part * grow
            top = new_top
            stats = put_lane(stats, level, here)
        stats = put_lane(stats, TOP_LANE, top)
        return stats, acc

    def middle_forward(which_levels, allowed_ref, codes_ref, acc_in, stats_in, *refs):
        count = len(which_levels)
        kv_refs, w_refs = refs[:count], refs[count : 2 * count]
        acc_ref, stats_ref = refs[2 * count :]
        key_pairs = [jnp.concatenate(key_parts(kv[:, :head]), axis=1) for kv in kv_refs]
        values = [with_ones(kv[:, head:]) for kv in kv_refs]
        for index in range(tiles):
            at = pl.ds(index * tile, tile)
            stats, acc = add_levels(
                which_levels, allowed_ref, codes_ref[at, :], stats_in[at, :], acc_in[at, :], key_pairs, values, w_refs, at
            )
            stats_ref[at, :] = stats
            acc_ref[at, :] = acc

    def last_forward(which_levels, allowed_ref, codes_ref, acc_in, stats_in, grad_ref, *refs):
        count = len(which_levels)
        kv_refs, w_refs = refs[:count], refs[count : 2 * count]
        out_ref, stats_ref = refs[2 * count :]
        key_pairs = [jnp.concatenate(key_parts(kv[:, :head]), axis=1) for kv in kv_refs]
        values = [with_ones(kv[:, head:]) for kv in kv_refs]
        for index in range(tiles):
            at = pl.ds(index * tile, tile)
            which, start = divmod(index * tile, tokens)
            columns = slice(which * head, (which + 1) * head)
            stats, acc = add_levels(
                which_levels, allowed_ref, codes_ref[at, :], stats_in[at, :], acc_in[at, :], key_pairs, values, w_refs, at
            )
            inverse = 1.0 / acc[:, head : head + 1]
            mixed = (acc[:, :head] * inverse).astype(bf16)
            out_ref[pl.ds(start, tile), columns] = mixed
            grad = grad_ref[pl.ds(start, tile), columns].astype(f32)
            delta = jnp.sum(grad * mixed.astype(f32), axis=1, keepdims=True)
            top = lane_of(stats, TOP_LANE)
            factor = lane_of(stats, FACTOR_LANE)
            shares = jnp.exp2((stats - top) * factor) * inverse
            lanes = lax.broadcasted_iota(jnp.int32, shares.shape, 1)
            open_lanes = lanes == levels
            for level in range(levels):
                open_lanes = open_lanes | ((lanes == level) & (allowed_ref[level] == 1))
            shares = jnp.where(open_lanes, shares, 0.0)
            stats_ref[at, :] = put_lane(shares, DELTA_LANE, delta)

    def backward(which_levels, first, last, *refs):
        count = len(which_levels)
        hat_ref, grad_ref, stats_ref = refs[:3]
        refs = refs[3:]
        if not first:
            dq_in, refs = refs[0], refs[1:]
        kv_refs, w_refs = refs[:count], refs[count : 2 * count]
        dq_ref = refs[2 * count]
        part_refs = refs[2 * count + 1 :]
        highs = [key_parts(kv[:, :head])[0] for kv in kv_refs]
        values = [with_ones(kv[:, head:]) for kv in kv_refs]
        dk = [None] * count
        dv = [None] * count
        lanes = lax.broadcasted_iota(jnp.int32, (tile, head), 1)
        for index in range(tiles):
            at = pl.ds(index * tile, tile)
            which, start = divmod(index * tile, tokens)
            columns = slice(which * head, (which + 1) * head)
            grad = grad_ref[pl.ds(start, tile), columns].astype(f32)
            stats = stats_ref[at, :]
            delta = lane_of(stats, DELTA_LANE) * (-2.0 / head)
            hat = hat_ref[at, :]
            dq = None if first else dq_in[at, :]
            for place, level in enumerate(which_levels):
                share = lane_of(stats, level)
                shared_grad = (grad * share).astype(bf16)
                offset = delta * share
                coarse = offset.astype(bf16)
                fine = (offset - coarse.astype(f32)).astype(bf16)
                extra = jnp.where(lanes < head // 2, coarse, fine)
                weights = w_refs[place][at, :]
                moved = dot_nt(jnp.concatenate([shared_grad, extra], axis=1), values[place])
                grad_scores = (weights.astype(f32) * moved).astype(bf16)
                add_q = dot_nn(grad_scores, highs[place])
                add_k = dot_tn(grad_scores, hat)
                add_v = dot_tn(weights, shared_grad)
                dq = add_q if dq is None else dq + add_q
                dk[place] = add_k if dk[place] is None else dk[place] + add_k
                dv[place] = add_v if dv[place] is None else dv[place] + add_v
            if last:
                dq_ref[pl.ds(start, tile), columns] = (dq * (score_scale / 127.0)).astype(bf16)
            else:
                dq_ref[at, :] = dq
        for place, part_ref in enumerate(part_refs):
            part_ref[:, :head] = (dk[place] * score_scale).astype(part_ref.dtype)
            part_ref[:, head:] = dv[place].astype(part_ref.dtype)

    def shape(*dims, dtype=f32):
        return jax.ShapeDtypeStruct(dims, dtype)

    def call(body, name, in_specs, outs):
        return pl.pallas_call(
            body, name=name, in_specs=in_specs, out_specs=tuple(vmem for _ in outs), out_shape=tuple(outs)
        )

    wide, narrow = shape(rows, tokens, dtype=bf16), shape(rows, head, dtype=bf16)
    acc, stats = shape(rows, 2 * head), shape(rows, 128)
    flat = shape(tokens, heads * head, dtype=bf16)

    def run_own(q, kv):
        return call(own_forward, "own_forward", [vmem] * 2, [narrow, narrow, wide, acc, stats])(q, kv)

    def run_middle(which_levels, allowed, codes, acc_in, stats_in, kvs):
        count = len(which_levels)

        def body(*refs):
            middle_forward(which_levels, *refs)

        return call(body, "middle_forward", [smem] + [vmem] * (3 + count), [wide] * count + [acc, stats])(
            allowed, codes, acc_in, stats_in, *kvs
        )

    def run_last(which_levels, allowed, codes, acc_in, stats_in, grad, kvs):
        count = len(which_levels)

        def body(*refs):
            last_forward(which_levels, *refs)

        return call(body, "last_forward", [smem] + [vmem] * (4 + count), [wide] * count + [flat, stats])(
            allowed, codes, acc_in, stats_in, grad, *kvs
        )

    def run_backward(which_levels, hat, grad, stats_in, dq, kvs, ws, last=False, dtype=bf16):
        count = len(which_levels)
        first = dq is None

        def body(*refs):
            backward(which_levels, first, last, *refs)

        ins = [hat, grad, stats_in] + ([] if first else [dq]) + list(kvs) + list(ws)
        outs = [flat if last else shape(rows, head)] + [shape(tokens, 2 * head, dtype=dtype)] * count
        return call(body, "backward", [vmem] * len(ins), outs)(*ins)

    return run_own, run_middle, run_last, run_backward


def local(queries, key_rows, value_rows, out_grad, link_mask):
    tokens, head = key_rows.shape
    heads = queries.shape[1] // head
    levels = link_mask.shape[1]
    group = 2 ** (levels - 2)
    half = group // 2
    far, near, mid = levels - 1, levels - 2, levels - 3
    run_own, run_middle, run_last, run_backward = make_kernels(tokens, head, heads, levels)
    block = lax.axis_index(AXES)
    distances = 2 ** jnp.arange(levels, dtype=jnp.int32)
    allowed = jnp.where(block >= distances, link_mask[0], 0)
    upper = (block % group) >= half

    own = jnp.concatenate([key_rows, value_rows], axis=1)
    kv = {near: shifted(own, group)}
    for level in range(mid):
        kv[level] = shifted(own, 2**level)
    codes, hat, w_own, acc, stats = run_own(queries, own)
    kv[far] = shifted(kv[near], group)
    kv[mid] = swapped(jnp.where(upper, kv[near], own), half)
    w = {levels: w_own}
    early = [near] + list(range(mid))
    *ws, acc, stats = run_middle(early, allowed, codes, acc, stats, [kv[level] for level in early])
    w.update(zip(early, ws))
    late = [far, mid]
    *ws, attention_out, stats = run_last(late, allowed, codes, acc, stats, out_grad, [kv[level] for level in late])
    w.update(zip(late, ws))

    def step(which, dq, **options):
        kvs = [own if level == levels else kv[level] for level in which]
        return run_backward(which, hat, out_grad, stats, dq, kvs, [w[level] for level in which], **options)

    dq, part_far = step([far], None)
    got_far = shifted(part_far, -group)
    dq, part_mid = step([mid], dq)
    got_mid = swapped(part_mid, half)
    back = []
    for level in range(mid):
        dq, part = step([level], dq)
        back.append(shifted(part, -(2**level)))
    query_grad, part_near, part_own = step([near, levels], dq, last=True, dtype=jnp.float32)
    through = part_near + got_far.astype(jnp.float32)
    got_mid = got_mid.astype(jnp.float32)
    through = through + jnp.where(upper, got_mid, 0.0)
    got_near = shifted(through.astype(jnp.bfloat16), -group)
    total = part_own + jnp.where(upper, 0.0, got_mid) + got_near.astype(jnp.float32)
    for part in back:
        total = total + part.astype(jnp.float32)
    total = total.astype(jnp.bfloat16)
    return attention_out, query_grad, total[:, :head], total[:, head:]


def solution(mesh):
    spec = P(AXES, None)
    return jax.shard_map(local, mesh=mesh, in_specs=(spec,) * 5, out_specs=(spec,) * 4, check_vma=False)
```

```python
import math

import jax
import jax.numpy as jnp
from jax import lax
from jax.experimental import pallas as pl
from jax.experimental.pallas import tpu as pltpu
from jax.sharding import PartitionSpec as P

AXES = ("row", "col")
SCALE_EPS = 1e-06
LOWEST = -3.0e38
TOP_LANE = 120
FACTOR_LANE = 121
DELTA_LANE = 122


def shifted(value, steps):
    count = lax.axis_size(AXES)
    first, last = max(0, -steps), min(count, count - steps)
    return lax.ppermute(value, AXES, [(source, source + steps) for source in range(first, last)])


def swapped(value, half):
    count = lax.axis_size(AXES)
    pairs = [(source, source + half if source % (2 * half) < half else source - half) for source in range(count)]
    return lax.ppermute(value, AXES, pairs)


def quantize(values):
    largest = jnp.max(jnp.abs(values), axis=-1, keepdims=True)
    scales = (largest + SCALE_EPS).astype(jnp.bfloat16).astype(jnp.float32)
    codes = jnp.clip(jnp.floor(values * (127.0 / scales) + 0.5), -127.0, 127.0)
    return codes, scales


def key_parts(keys):
    codes, scales = quantize(keys.astype(jnp.float32))
    exact = codes * scales
    high = exact.astype(jnp.bfloat16)
    low = (exact - high.astype(jnp.float32)).astype(jnp.bfloat16)
    return high, low


def dot_nt(left, right):
    return lax.dot_general(left, right, (((1,), (1,)), ((), ())), preferred_element_type=jnp.float32)


def dot_nn(left, right):
    return lax.dot_general(left, right, (((1,), (0,)), ((), ())), preferred_element_type=jnp.float32)


def dot_tn(left, right):
    return lax.dot_general(left, right, (((0,), (0,)), ((), ())), preferred_element_type=jnp.float32)


def with_ones(values):
    return jnp.concatenate([values, jnp.ones_like(values)], axis=1)


def lane_of(stats, lane):
    return stats[:, lane : lane + 1]


def put_lane(stats, lane, column):
    lanes = lax.broadcasted_iota(jnp.int32, stats.shape, 1)
    return jnp.where(lanes == lane, column, stats)


def level_scores(codes, key_pair):
    return dot_nt(jnp.concatenate([codes, codes], axis=1), key_pair)


def make_kernels(tokens, head, heads, levels):
    rows = tokens * heads
    tile = min(256, tokens)
    tiles = rows // tile
    score_factor = math.log2(math.e) / (127.0 * 127.0 * math.sqrt(head))
    score_scale = 1.0 / math.sqrt(head)
    vmem = pl.BlockSpec(memory_space=pltpu.VMEM)
    smem = pl.BlockSpec(memory_space=pltpu.SMEM)
    f32, bf16 = jnp.float32, jnp.bfloat16

    def own_forward(q_ref, kv_ref, codes_ref, hat_ref, w_ref, acc_ref, stats_ref):
        high, low = key_parts(kv_ref[:, :head])
        key_pair = jnp.concatenate([high, low], axis=1)
        values = with_ones(kv_ref[:, head:])
        for index in range(tiles):
            at = pl.ds(index * tile, tile)
            which, start = divmod(index * tile, tokens)
            raw = q_ref[pl.ds(start, tile), which * head : (which + 1) * head].astype(f32)
            codes, scales = quantize(raw)
            hat_ref[at, :] = (codes * (scales / 127.0)).astype(bf16)
            codes = codes.astype(bf16)
            codes_ref[at, :] = codes
            factor = scales * score_factor
            scores = level_scores(codes, key_pair)
            t = lax.broadcasted_iota(jnp.int32, scores.shape, 0) + start
            u = lax.broadcasted_iota(jnp.int32, scores.shape, 1)
            scores = jnp.where(u <= t, scores, LOWEST)
            top = jnp.max(scores, axis=1, keepdims=True)
            weights = jnp.exp2((scores - top) * factor).astype(bf16)
            w_ref[at, :] = weights
            acc_ref[at, :] = dot_nn(weights, values)
            stats = jnp.zeros((tile, 128), f32)
            stats = put_lane(stats, levels, top)
            stats = put_lane(stats, TOP_LANE, top)
            stats = put_lane(stats, FACTOR_LANE, factor)
            stats_ref[at, :] = stats

    def add_levels(which_levels, allowed_ref, codes, stats, acc, key_pairs, values, w_refs, at):
        factor = lane_of(stats, FACTOR_LANE)
        top = lane_of(stats, TOP_LANE)
        for level, key_pair, value, w_ref in zip(which_levels, key_pairs, values, w_refs):
            scores = level_scores(codes, key_pair)
            here = jnp.max(scores, axis=1, keepdims=True)
            weights = jnp.exp2((scores - here) * factor).astype(bf16)
            w_ref[at, :] = weights
            part = dot_nn(weights, value)
            allowed = allowed_ref[level] == 1
            new_top = jnp.maximum(top, jnp.where(allowed, here, LOWEST))
            grow = jnp.where(allowed, jnp.exp2((here - new_top) * factor), 0.0)
            acc = acc * jnp.exp2((top - new_top) * factor) + part * grow
            top = new_top
            stats = put_lane(stats, level, here)
        stats = put_lane(stats, TOP_LANE, top)
        return stats, acc

    def middle_forward(which_levels, allowed_ref, codes_ref, acc_in, stats_in, *refs):
        count = len(which_levels)
        kv_refs, w_refs = refs[:count], refs[count : 2 * count]
        acc_ref, stats_ref = refs[2 * count :]
        key_pairs = [jnp.concatenate(key_parts(kv[:, :head]), axis=1) for kv in kv_refs]
        values = [with_ones(kv[:, head:]) for kv in kv_refs]
        for index in range(tiles):
            at = pl.ds(index * tile, tile)
            stats, acc = add_levels(
                which_levels, allowed_ref, codes_ref[at, :], stats_in[at, :], acc_in[at, :], key_pairs, values, w_refs, at
            )
            stats_ref[at, :] = stats
            acc_ref[at, :] = acc

    def last_forward(which_levels, allowed_ref, codes_ref, acc_in, stats_in, grad_ref, *refs):
        count = len(which_levels)
        kv_refs, w_refs = refs[:count], refs[count : 2 * count]
        out_ref, stats_ref = refs[2 * count :]
        key_pairs = [jnp.concatenate(key_parts(kv[:, :head]), axis=1) for kv in kv_refs]
        values = [with_ones(kv[:, head:]) for kv in kv_refs]
        for index in range(tiles):
            at = pl.ds(index * tile, tile)
            which, start = divmod(index * tile, tokens)
            columns = slice(which * head, (which + 1) * head)
            stats, acc = add_levels(
                which_levels, allowed_ref, codes_ref[at, :], stats_in[at, :], acc_in[at, :], key_pairs, values, w_refs, at
            )
            inverse = 1.0 / acc[:, head : head + 1]
            mixed = (acc[:, :head] * inverse).astype(bf16)
            out_ref[pl.ds(start, tile), columns] = mixed
            grad = grad_ref[pl.ds(start, tile), columns].astype(f32)
            delta = jnp.sum(grad * mixed.astype(f32), axis=1, keepdims=True)
            top = lane_of(stats, TOP_LANE)
            factor = lane_of(stats, FACTOR_LANE)
            shares = jnp.exp2((stats - top) * factor) * inverse
            lanes = lax.broadcasted_iota(jnp.int32, shares.shape, 1)
            open_lanes = lanes == levels
            for level in range(levels):
                open_lanes = open_lanes | ((lanes == level) & (allowed_ref[level] == 1))
            shares = jnp.where(open_lanes, shares, 0.0)
            stats_ref[at, :] = put_lane(shares, DELTA_LANE, delta)

    def backward(which_levels, first, last, *refs):
        count = len(which_levels)
        hat_ref, grad_ref, stats_ref = refs[:3]
        refs = refs[3:]
        if not first:
            dq_in, refs = refs[0], refs[1:]
        kv_refs, w_refs = refs[:count], refs[count : 2 * count]
        dq_ref = refs[2 * count]
        part_refs = refs[2 * count + 1 :]
        highs = [key_parts(kv[:, :head])[0] for kv in kv_refs]
        values = [with_ones(kv[:, head:]) for kv in kv_refs]
        dk = [None] * count
        dv = [None] * count
        lanes = lax.broadcasted_iota(jnp.int32, (tile, head), 1)
        for index in range(tiles):
            at = pl.ds(index * tile, tile)
            which, start = divmod(index * tile, tokens)
            columns = slice(which * head, (which + 1) * head)
            grad = grad_ref[pl.ds(start, tile), columns].astype(f32)
            stats = stats_ref[at, :]
            delta = lane_of(stats, DELTA_LANE) * (-2.0 / head)
            hat = hat_ref[at, :]
            dq = None if first else dq_in[at, :]
            for place, level in enumerate(which_levels):
                share = lane_of(stats, level)
                shared_grad = (grad * share).astype(bf16)
                offset = delta * share
                coarse = offset.astype(bf16)
                fine = (offset - coarse.astype(f32)).astype(bf16)
                extra = jnp.where(lanes < head // 2, coarse, fine)
                weights = w_refs[place][at, :]
                moved = dot_nt(jnp.concatenate([shared_grad, extra], axis=1), values[place])
                grad_scores = (weights.astype(f32) * moved).astype(bf16)
                add_q = dot_nn(grad_scores, highs[place])
                add_k = dot_tn(grad_scores, hat)
                add_v = dot_tn(weights, shared_grad)
                dq = add_q if dq is None else dq + add_q
                dk[place] = add_k if dk[place] is None else dk[place] + add_k
                dv[place] = add_v if dv[place] is None else dv[place] + add_v
            if last:
                dq_ref[pl.ds(start, tile), columns] = (dq * (score_scale / 127.0)).astype(bf16)
            else:
                dq_ref[at, :] = dq
        for place, part_ref in enumerate(part_refs):
            part_ref[:, :head] = (dk[place] * score_scale).astype(part_ref.dtype)
            part_ref[:, head:] = dv[place].astype(part_ref.dtype)

    def shape(*dims, dtype=f32):
        return jax.ShapeDtypeStruct(dims, dtype)

    def call(body, name, in_specs, outs):
        run = pl.pallas_call(
            body,
            name=name,
            in_specs=in_specs,
            out_specs=tuple(vmem for _ in outs),
            out_shape=tuple(pltpu.VMEM(out.shape, out.dtype) for out in outs),
            compiler_params=pltpu.CompilerParams(vmem_limit_bytes=16 * 2**20),
        )

        def placed(*operands):
            return run(
                *(
                    pltpu.with_memory_space_constraint(operand, pltpu.VMEM) if spec is vmem else operand
                    for spec, operand in zip(in_specs, operands)
                )
            )

        return placed

    wide, narrow = shape(rows, tokens, dtype=bf16), shape(rows, head, dtype=bf16)
    acc, stats = shape(rows, 2 * head), shape(rows, 128)
    flat = shape(tokens, heads * head, dtype=bf16)

    def run_own(q, kv):
        return call(own_forward, "own_forward", [vmem] * 2, [narrow, narrow, wide, acc, stats])(q, kv)

    def run_middle(which_levels, allowed, codes, acc_in, stats_in, kvs):
        count = len(which_levels)

        def body(*refs):
            middle_forward(which_levels, *refs)

        return call(body, "middle_forward", [smem] + [vmem] * (3 + count), [wide] * count + [acc, stats])(
            allowed, codes, acc_in, stats_in, *kvs
        )

    def run_last(which_levels, allowed, codes, acc_in, stats_in, grad, kvs):
        count = len(which_levels)

        def body(*refs):
            last_forward(which_levels, *refs)

        return call(body, "last_forward", [smem] + [vmem] * (4 + count), [wide] * count + [flat, stats])(
            allowed, codes, acc_in, stats_in, grad, *kvs
        )

    def run_backward(which_levels, hat, grad, stats_in, dq, kvs, ws, last=False, dtype=bf16):
        count = len(which_levels)
        first = dq is None

        def body(*refs):
            backward(which_levels, first, last, *refs)

        ins = [hat, grad, stats_in] + ([] if first else [dq]) + list(kvs) + list(ws)
        outs = [flat if last else shape(rows, head)] + [shape(tokens, 2 * head, dtype=dtype)] * count
        return call(body, "backward", [vmem] * len(ins), outs)(*ins)

    return run_own, run_middle, run_last, run_backward


def local(queries, key_rows, value_rows, out_grad, link_mask):
    tokens, head = key_rows.shape
    heads = queries.shape[1] // head
    levels = link_mask.shape[1]
    group = 2 ** (levels - 2)
    half = group // 2
    far, near, mid = levels - 1, levels - 2, levels - 3
    run_own, run_middle, run_last, run_backward = make_kernels(tokens, head, heads, levels)
    block = lax.axis_index(AXES)
    distances = 2 ** jnp.arange(levels, dtype=jnp.int32)
    allowed = jnp.where(block >= distances, link_mask[0], 0)
    upper = (block % group) >= half

    own = jnp.concatenate([key_rows, value_rows], axis=1)
    kv = {near: shifted(own, group)}
    for level in range(mid):
        kv[level] = shifted(own, 2**level)
    codes, hat, w_own, acc, stats = run_own(queries, own)
    kv[far] = shifted(kv[near], group)
    kv[mid] = swapped(jnp.where(upper, kv[near], own), half)
    w = {levels: w_own}
    early = [near] + list(range(mid))
    *ws, acc, stats = run_middle(early, allowed, codes, acc, stats, [kv[level] for level in early])
    w.update(zip(early, ws))
    late = [far, mid]
    *ws, attention_out, stats = run_last(late, allowed, codes, acc, stats, out_grad, [kv[level] for level in late])
    w.update(zip(late, ws))

    def step(which, dq, **options):
        kvs = [own if level == levels else kv[level] for level in which]
        return run_backward(which, hat, out_grad, stats, dq, kvs, [w[level] for level in which], **options)

    dq, part_far = step([far], None)
    got_far = shifted(part_far, -group)
    dq, part_mid = step([mid], dq)
    got_mid = swapped(part_mid, half)
    back = []
    for level in range(mid):
        dq, part = step([level], dq)
        back.append(shifted(part, -(2**level)))
    query_grad, part_near, part_own = step([near, levels], dq, last=True, dtype=jnp.float32)
    through = part_near + got_far.astype(jnp.float32)
    got_mid = got_mid.astype(jnp.float32)
    through = through + jnp.where(upper, got_mid, 0.0)
    got_near = shifted(through.astype(jnp.bfloat16), -group)
    total = part_own + jnp.where(upper, 0.0, got_mid) + got_near.astype(jnp.float32)
    for part in back:
        total = total + part.astype(jnp.float32)
    total = total.astype(jnp.bfloat16)
    return attention_out, query_grad, total[:, :head], total[:, head:]


def solution(mesh):
    spec = P(AXES, None)
    return jax.shard_map(local, mesh=mesh, in_specs=(spec,) * 5, out_specs=(spec,) * 4, check_vma=False)
```
